32 devices in a mesh: ctx: 16 (over z, x, core), head: 2 (over y).
Axes of the slice: x: 2, y: 2, z: 4, core: 2. Of those that a mesh axis runs over, the one named last changes fastest.
Arguments:
- query_heads: bfloat16 [2048, 64, 576], P('ctx', 'head'), may hold values from -16 to 16
- key_latent: bfloat16 [2048, 576], P('ctx'), may hold values from -6 to 6
- doc_start: int32 [2048], P('ctx'), may hold values from 0 to 2047, as said below
- out_grad: bfloat16 [2048, 64, 512], P('ctx', 'head'), may hold values from -12 to 12
Outputs:
- attention: bfloat16 [2048, 64, 512], P('ctx', 'head')
- d_query: bfloat16 [2048, 64, 576], P('ctx', 'head')
- d_key: float32 [2048, 576], P(('ctx', 'head'))
The draws below stay inside these ranges and needn't reach their ends.
Inputs may be any that keep to these rules, and one draw needn't show every extreme that they name: doc_start[t] <= t; doc_start[t] is t or doc_start[t - 1]; every document holds at most 256 tokens, and some document holds exactly 256.
All inputs are finite; a program needn't handle non-finite values.
Results may differ from the reference program's by a relative error of at most 0.013.
Values may be sent and summed in bfloat16 or wider, within the bound.
A program may use at most 128 MiB of HBM per device.

```python
import jax
import jax.numpy as jnp
from jax import lax

HEADS = 64
LAT = 512
MAXDOC = 256
TOK_DEV = 128
DQK = 576
TOKENS = 2048


def common_draw(key):
    positions = jnp.arange(TOKENS, dtype=jnp.int32)
    choose = jax.random.randint(jax.random.fold_in(key, 11), (TOKENS,), 0, 2)
    longer = jax.random.randint(jax.random.fold_in(key, 12), (TOKENS,), MAXDOC // 2, MAXDOC + 1)
    shorter = jax.random.randint(jax.random.fold_in(key, 13), (TOKENS,), 1, MAXDOC // 8 + 1)
    forced = jax.random.randint(jax.random.fold_in(key, 14), (), 0, 4)
    lengths = jnp.where(choose == 0, longer, shorter)
    lengths = jnp.where(positions == forced, MAXDOC, lengths).astype(jnp.int32)
    endings = jnp.cumsum(lengths).astype(jnp.int32)
    beginnings = endings - lengths
    doc_index = jnp.searchsorted(endings, positions, side='right').astype(jnp.int32)
    doc_first = beginnings[doc_index].astype(jnp.int32)
    key_rows = jnp.clip(jax.random.normal(jax.random.fold_in(key, 21), (TOKENS, DQK), jnp.float32), -6.0, 6.0)
    queries = jnp.clip(jax.random.normal(jax.random.fold_in(key, 23), (TOKENS, HEADS, DQK), jnp.float32), -6.0, 6.0)
    return (doc_first, queries, key_rows)


def draw_query_heads(key, part):
    return common_draw(key)[1].astype(jnp.bfloat16)


def draw_key_latent(key, part):
    return common_draw(key)[2].astype(jnp.bfloat16)


def draw_doc_start(key, part):
    return common_draw(key)[0].astype(jnp.int32)


def level_of(own_key, dims, pieces, least, high):
    def one(position, parts):
        heights = jax.random.uniform(jax.random.fold_in(jax.random.fold_in(own_key, 6), position), (parts,), jnp.float32, least / len(pieces), high / len(pieces))
        return jnp.repeat(jnp.exp(heights), dims[position] // parts).reshape((-1,) + (1,) * (len(dims) - position - 1))

    loudness = one(*pieces[0])
    for cut in pieces[1:]:
        loudness = loudness * one(*cut)
    return loudness


def gaussian(rng, shape, spread, limit, cuts=(), held_as=jnp.bfloat16):
    loudness = level_of(rng, shape, cuts, -0.22, 0.18) if cuts else 1.0
    entries = jax.random.normal(rng, shape, jnp.float32) * spread * loudness
    return jnp.minimum(jnp.maximum(entries, -limit), limit).astype(held_as)


def setup_inputs(seed: int = 0) -> dict:
    keys = jax.random.split(jax.random.key(seed), 5)
    query_heads = draw_query_heads(jax.random.fold_in(keys[4], 71), 0)
    key_latent = draw_key_latent(jax.random.fold_in(keys[4], 71), 0)
    doc_start = draw_doc_start(jax.random.fold_in(keys[4], 71), 0)
    out_grad = gaussian(keys[3], (TOKENS, HEADS, LAT), 2.0, 12.0, ((0, 16), (1, 2)))
    return dict(query_heads=query_heads, key_latent=key_latent, doc_start=doc_start, out_grad=out_grad)


score_scale = 192 ** -0.5


def reference(query_heads, key_latent, doc_start, out_grad):
    reach = (MAXDOC + TOK_DEV - 2) // TOK_DEV
    span = (reach + 1) * TOK_DEV
    block_count = TOKENS // TOK_DEV
    padded = jnp.concatenate([jnp.zeros((reach * TOK_DEV, DQK), jnp.bfloat16), key_latent], axis=0)

    def one_block(carried, block_index):
        start = (block_index * TOK_DEV).astype(jnp.int32)
        window = lax.dynamic_slice_in_dim(padded, start, span, 0).astype(jnp.float32)
        queries = lax.dynamic_slice_in_dim(query_heads, start, TOK_DEV, 0).astype(jnp.float32)
        cotangent = lax.dynamic_slice_in_dim(out_grad, start, TOK_DEV, 0).astype(jnp.float32)
        doc_first = lax.dynamic_slice_in_dim(doc_start, start, TOK_DEV, 0)
        query_pos = start + jnp.arange(TOK_DEV, dtype=jnp.int32)
        key_pos = start - reach * TOK_DEV + jnp.arange(span, dtype=jnp.int32)
        visible = (key_pos[None, :] >= doc_first[:, None]) & (key_pos[None, :] <= query_pos[:, None])
        scores = jnp.einsum("thd,kd->thk", queries, window) * score_scale
        scores = jnp.where(visible[:, None, :], scores, -jnp.inf)
        top = jnp.max(scores, axis=2, keepdims=True)
        expon = jnp.exp(scores - top)
        probs = expon / jnp.sum(expon, axis=2, keepdims=True)
        weights = probs.astype(jnp.bfloat16).astype(jnp.float32)
        values = window[:, :LAT]
        attention = jnp.einsum("thk,kc->thc", weights, values).astype(jnp.bfloat16)
        dprob = jnp.einsum("thc,kc->thk", cotangent, values)
        row_delta = jnp.sum(probs * dprob, axis=2, keepdims=True)
        dscore = (score_scale * probs * (dprob - row_delta)).astype(jnp.bfloat16).astype(jnp.float32)
        d_query = jnp.einsum("thk,kd->thd", dscore, window).astype(jnp.bfloat16)
        from_scores = jnp.einsum("thk,thd->kd", dscore, queries)
        from_values = jnp.einsum("thk,thc->kc", weights, cotangent)
        window_grad = from_scores + jnp.pad(from_values, ((0, 0), (0, DQK - LAT)))
        current = lax.dynamic_slice_in_dim(carried, start, span, 0)
        carried = lax.dynamic_update_slice_in_dim(carried, current + window_grad, start, 0)
        return carried, (attention, d_query)

    initial = jnp.zeros((reach * TOK_DEV + TOKENS, DQK), jnp.float32)
    summed, (attention, d_query) = lax.scan(one_block, initial, jnp.arange(block_count, dtype=jnp.int32))
    attention = attention.reshape(TOKENS, HEADS, LAT)
    d_query = d_query.reshape(TOKENS, HEADS, DQK)
    d_key = summed[reach * TOK_DEV:]
    return attention, d_query, d_key
```

```python
from functools import partial

import jax
import jax.numpy as jnp
from jax import lax
from jax.experimental import pallas as pl
from jax.experimental.pallas import tpu as pltpu
from jax.sharding import PartitionSpec as P

MAXDOC = 256
LANES = 128
ALIGN = 16

score_scale = 192 ** (-0.5)
log2_e = 1.4426950408889634


def shifted(value, axis, steps):
    count = lax.axis_size(axis)
    return lax.ppermute(value, axis, [(source, source + steps) for source in range(count - steps)])


def dot(left, right, dims):
    return lax.dot_general(left, right, (dims, ((), ())), preferred_element_type=jnp.float32)


def window(first_ref, tokens, reach_rows, span, tile):
    origin = lax.axis_index("ctx") * (first_ref.shape[0]) - reach_rows
    low = (first_ref[tile * tokens] - origin) // ALIGN * ALIGN
    need = reach_rows + (tile + 1) * tokens - low
    return origin, low, need


def for_width(first_ref, tokens, reach_rows, span, tile, body):
    origin, low, need = window(first_ref, tokens, reach_rows, span, tile)
    for width in range(LANES, span + 1, LANES):
        fits = need <= width
        if width == LANES:
            chosen = fits
        elif width == span:
            chosen = need > width - LANES
        else:
            chosen = fits & (need > width - LANES)

        @pl.when(chosen)
        def _(width=width):
            start = pl.multiple_of(jnp.minimum(low, span - width), ALIGN)
            body(origin, start, width)


def probs_and_grads(first_ref, q, g, keys, bias_ref, tokens, heads, reach_rows, tile, origin, start, width):
    latent = g.shape[1]
    column = lax.broadcasted_iota(jnp.int32, (1, width), 1) + start
    for t in range(tokens):
        first = first_ref[tile * tokens + t] - origin
        own = reach_rows + tile * tokens + t
        seen = (column >= first) & (column <= own)
        bias_ref[pl.ds(t, 1), :width] = jnp.where(seen, 0.0, -jnp.inf)
    scores = dot(q, keys, ((1,), (1,))) * (score_scale * log2_e)
    scores = scores.reshape(tokens, heads, width) + bias_ref[:, :width][:, None, :]
    scores = scores.reshape(tokens * heads, width)
    top = jnp.max(scores, axis=1, keepdims=True)
    expon = jnp.exp2(scores - top)
    probs = expon * (1.0 / jnp.sum(expon, axis=1, keepdims=True))
    weights = probs.astype(jnp.bfloat16)
    dprob = dot(g, keys[:, :latent], ((1,), (1,)))
    delta = jnp.sum(probs * dprob, axis=1, keepdims=True)
    dscore = (score_scale * probs * (dprob - delta)).astype(jnp.bfloat16)
    return weights, dscore


def whole_kernel(tokens, heads, reach_rows, first_ref, q_ref, g_ref, k_ref, att_ref, dq_ref, dk_ref, bias_ref, acc_ref):
    tile = pl.program_id(0)
    span = k_ref.shape[0]
    latent = g_ref.shape[1]

    @pl.when(tile == 0)
    def _():
        acc_ref[...] = jnp.zeros_like(acc_ref)

    def body(origin, start, width):
        q = q_ref[...]
        g = g_ref[...]
        rows = pl.ds(start, width)
        keys = k_ref[rows, :]
        weights, dscore = probs_and_grads(
            first_ref, q, g, keys, bias_ref, tokens, heads, reach_rows, tile, origin, start, width
        )
        acc_ref[rows, :] += dot(dscore, q, ((0,), (0,)))
        acc_ref[rows, :latent] += dot(weights, g, ((0,), (0,)))
        att_ref[...] = dot(weights, keys[:, :latent], ((1,), (0,))).astype(att_ref.dtype)
        dq_ref[...] = dot(dscore, keys, ((1,), (0,))).astype(dq_ref.dtype)

    for_width(first_ref, tokens, reach_rows, span, tile, body)

    @pl.when(tile == pl.num_programs(0) - 1)
    def _():
        dk_ref[...] = acc_ref[...].astype(dk_ref.dtype)


def attend(q, g, keys, doc_start, heads, tokens):
    rows, width = q.shape
    latent = g.shape[1]
    span = keys.shape[0]
    block_rows = doc_start.shape[0]
    tile_rows = tokens * heads
    row_spec = lambda columns: pl.BlockSpec((tile_rows, columns), lambda i, first: (i, 0))
    full = pl.BlockSpec((span, width), lambda i, first: (0, 0))
    return pl.pallas_call(
        partial(whole_kernel, tokens, heads, span - block_rows),
        grid_spec=pltpu.PrefetchScalarGridSpec(
            num_scalar_prefetch=1,
            grid=(block_rows // tokens,),
            in_specs=[row_spec(width), row_spec(latent), full],
            out_specs=[row_spec(latent), row_spec(width), full],
            scratch_shapes=[
                pltpu.VMEM((tokens, span), jnp.float32),
                pltpu.VMEM((span, width), jnp.float32),
            ],
        ),
        out_shape=[
            jax.ShapeDtypeStruct((rows, latent), jnp.bfloat16),
            jax.ShapeDtypeStruct((rows, width), jnp.bfloat16),
            jax.ShapeDtypeStruct((span, width), jnp.bfloat16),
        ],
        compiler_params=pltpu.CompilerParams(
            dimension_semantics=("arbitrary",), vmem_limit_bytes=60 * 1024 * 1024
        ),
        name="attend",
    )(doc_start, q, g, keys)


def exchange(partials, block_rows, reach):
    ctx_count = lax.axis_size("ctx")
    head_count = lax.axis_size("head")
    head_index = lax.axis_index("head")
    own_rows = block_rows // head_count
    total = None
    for offset in range(reach, -1, -1):
        for turn in range(head_count - 1, -1, -1):
            target = (head_index + turn) % head_count
            piece = lax.dynamic_slice_in_dim(
                partials, (reach - offset) * block_rows + target * own_rows, own_rows, 0
            )
            if offset or turn:
                pairs = [
                    (c * head_count + h, (c - offset) * head_count + (h + turn) % head_count)
                    for c in range(offset, ctx_count)
                    for h in range(head_count)
                ]
                piece = lax.ppermute(piece, ("ctx", "head"), pairs)
            piece = piece.astype(jnp.float32)
            total = piece if total is None else total + piece
    return total


def shards(query_heads, key_latent, doc_start, out_grad):
    block_rows, head_count, width = query_heads.shape
    latent = out_grad.shape[2]
    reach = (MAXDOC + block_rows - 2) // block_rows
    keys = jnp.concatenate(
        [shifted(key_latent, "ctx", offset) for offset in range(reach, 0, -1)] + [key_latent], axis=0
    )
    rows = block_rows * head_count
    attention, d_query, partials = attend(
        query_heads.reshape(rows, width),
        out_grad.reshape(rows, latent),
        keys,
        doc_start,
        head_count,
        32,
    )
    d_key = exchange(partials, block_rows, reach)
    return (
        attention.reshape(block_rows, head_count, latent),
        d_query.reshape(block_rows, head_count, width),
        d_key,
    )


def solution(mesh):
    return jax.shard_map(
        shards,
        mesh=mesh,
        in_specs=(P("ctx", "head", None), P("ctx", None), P("ctx"), P("ctx", "head", None)),
        out_specs=(P("ctx", "head", None), P("ctx", "head", None), P(("ctx", "head"), None)),
        check_vma=False,
    )
```

```python
from functools import partial

import jax
import jax.numpy as jnp
from jax import lax
from jax.experimental import pallas as pl
from jax.experimental.pallas import tpu as pltpu
from jax.sharding import PartitionSpec as P

MAXDOC = 256
LANES = 128
ALIGN = 16

score_scale = 192 ** (-0.5)
log2_e = 1.4426950408889634


def dot(left, right, dims):
    return lax.dot_general(left, right, (dims, ((), ())), preferred_element_type=jnp.float32)


def window(first_ref, tokens, reach_rows, span, tile):
    origin = lax.axis_index("ctx") * (first_ref.shape[0]) - reach_rows
    low = (first_ref[tile * tokens] - origin) // ALIGN * ALIGN
    need = reach_rows + (tile + 1) * tokens - low
    return origin, low, need


def for_width(first_ref, tokens, reach_rows, span, tile, body):
    origin, low, need = window(first_ref, tokens, reach_rows, span, tile)
    for width in range(LANES, span + 1, LANES):
        fits = need <= width
        if width == LANES:
            chosen = fits
        elif width == span:
            chosen = need > width - LANES
        else:
            chosen = fits & (need > width - LANES)

        @pl.when(chosen)
        def _(width=width):
            start = pl.multiple_of(jnp.minimum(low, span - width), ALIGN)
            body(origin, start, width)


def probs_and_grads(first_ref, q, g, keys, bias_ref, tokens, heads, reach_rows, tile, origin, start, width):
    latent = g.shape[1]
    column = lax.broadcasted_iota(jnp.int32, (1, width), 1) + start
    for t in range(tokens):
        first = first_ref[tile * tokens + t] - origin
        own = reach_rows + tile * tokens + t
        seen = (column >= first) & (column <= own)
        bias_ref[pl.ds(t, 1), :width] = jnp.where(seen, 0.0, -jnp.inf)
    scores = dot(q, keys, ((1,), (1,))) * (score_scale * log2_e)
    scores = scores.reshape(tokens, heads, width) + bias_ref[:, :width][:, None, :]
    scores = scores.reshape(tokens * heads, width)
    top = jnp.max(scores, axis=1, keepdims=True)
    expon = jnp.exp2(scores - top)
    probs = expon * (1.0 / jnp.sum(expon, axis=1, keepdims=True))
    weights = probs.astype(jnp.bfloat16)
    dprob = dot(g, keys[:, :latent], ((1,), (1,)))
    delta = jnp.sum(probs * dprob, axis=1, keepdims=True)
    dscore = (score_scale * probs * (dprob - delta)).astype(jnp.bfloat16)
    return weights, dscore


def whole_kernel(tokens, heads, reach_rows, first_ref, q_ref, g_ref, k_ref, att_ref, dq_ref, dk_ref, bias_ref, acc_ref):
    tile = pl.program_id(0)
    span = k_ref.shape[0]
    latent = g_ref.shape[1]

    @pl.when(tile == 0)
    def _():
        acc_ref[...] = jnp.zeros_like(acc_ref)

    def body(origin, start, width):
        q = q_ref[...]
        g = g_ref[...]
        rows = pl.ds(start, width)
        keys = k_ref[rows, :]
        weights, dscore = probs_and_grads(
            first_ref, q, g, keys, bias_ref, tokens, heads, reach_rows, tile, origin, start, width
        )
        acc_ref[rows, :] += dot(dscore, q, ((0,), (0,)))
        acc_ref[rows, :latent] += dot(weights, g, ((0,), (0,)))
        att_ref[...] = dot(weights, keys[:, :latent], ((1,), (0,))).astype(att_ref.dtype)
        dq_ref[...] = dot(dscore, keys, ((1,), (0,))).astype(dq_ref.dtype)

    for_width(first_ref, tokens, reach_rows, span, tile, body)

    @pl.when(tile == pl.num_programs(0) - 1)
    def _():
        dk_ref[...] = acc_ref[...].astype(dk_ref.dtype)


def attend(q, g, keys, doc_start, heads, tokens):
    rows, width = q.shape
    latent = g.shape[1]
    span = keys.shape[0]
    block_rows = doc_start.shape[0]
    tile_rows = tokens * heads
    row_spec = lambda columns: pl.BlockSpec((tile_rows, columns), lambda i, first: (i, 0))
    full = pl.BlockSpec((span, width), lambda i, first: (0, 0))
    return pl.pallas_call(
        partial(whole_kernel, tokens, heads, span - block_rows),
        grid_spec=pltpu.PrefetchScalarGridSpec(
            num_scalar_prefetch=1,
            grid=(block_rows // tokens,),
            in_specs=[row_spec(width), row_spec(latent), full],
            out_specs=[row_spec(latent), row_spec(width), full],
            scratch_shapes=[
                pltpu.VMEM((tokens, span), jnp.float32),
                pltpu.VMEM((span, width), jnp.float32),
            ],
        ),
        out_shape=[
            jax.ShapeDtypeStruct((rows, latent), jnp.bfloat16),
            jax.ShapeDtypeStruct((rows, width), jnp.bfloat16),
            jax.ShapeDtypeStruct((span, width), jnp.bfloat16),
        ],
        compiler_params=pltpu.CompilerParams(
            dimension_semantics=("arbitrary",), vmem_limit_bytes=60 * 1024 * 1024
        ),
        name="attend",
    )(doc_start, q, g, keys)


def at(ctx_index, head_index):
    return {"ctx": ctx_index, "head": head_index}


def greet(partners):
    barrier = pltpu.get_barrier_semaphore()
    for present, place in partners:

        @pl.when(present)
        def _(place=place):
            pl.semaphore_signal(
                barrier, inc=1, device_id=place, device_id_type=pl.DeviceIdType.MESH
            )

    pl.semaphore_wait(barrier, sum(jnp.where(present, 1, 0) for present, _ in partners))


def unit(size):
    row = lax.broadcasted_iota(jnp.int32, (size, size), 0)
    column = lax.broadcasted_iota(jnp.int32, (size, size), 1)
    return (row == column).astype(jnp.bfloat16)


def gather_kernel(reach, count, k_ref, q_ref, keys_ref, out_ref, held, turned, send_sem, recv_sem):
    step = pl.program_id(0)
    me = lax.axis_index("ctx")
    head = lax.axis_index("head")
    group, width, tokens = q_ref.shape

    def copy(offset):
        return pltpu.make_async_remote_copy(
            src_ref=k_ref,
            dst_ref=held.at[offset - 1],
            send_sem=send_sem.at[offset - 1],
            recv_sem=recv_sem.at[offset - 1],
            device_id=at(jnp.minimum(me + offset, count - 1), head),
            device_id_type=pl.DeviceIdType.MESH,
        )

    offsets = range(1, reach + 1)

    @pl.when(step == 0)
    def _():
        greet(
            [(me + offset < count, at(jnp.minimum(me + offset, count - 1), head)) for offset in offsets]
            + [(me >= offset, at(jnp.maximum(me - offset, 0), head)) for offset in offsets]
        )
        for offset in offsets:

            @pl.when(me + offset < count)
            def _(offset=offset):
                copy(offset).start()

    eye = unit(tokens)
    for h in range(group):
        rows = dot(eye, q_ref[h], ((1,), (1,)))
        for c in range(pl.cdiv(width, LANES)):
            size = min(LANES, width - c * LANES)
            part = rows[:, c * LANES : c * LANES + size]
            if size < LANES:
                part = jnp.concatenate([part, jnp.zeros((tokens, LANES - size), jnp.float32)], axis=1)
            turned[c, pl.ds(h, tokens, stride=group), :] = part
    for c in range(pl.cdiv(width, LANES)):
        size = min(LANES, width - c * LANES)
        part = turned[c].reshape(tokens, group, LANES).astype(jnp.bfloat16)
        out_ref[:, :, c * LANES : c * LANES + size] = part[:, :, :size]

    @pl.when(step == pl.num_programs(0) - 1)
    def _():
        keys_ref[reach * tokens :, :] = dot(eye, k_ref[...], ((1,), (1,))).astype(jnp.bfloat16)
        for offset in offsets:
            place = pl.ds((reach - offset) * tokens, tokens)

            @pl.when(me >= offset)
            def _(offset=offset, place=place):
                copy(offset).wait_recv()
                keys_ref[place, :] = dot(eye, held[offset - 1], ((1,), (1,))).astype(jnp.bfloat16)

            @pl.when(me < offset)
            def _(place=place):
                keys_ref[place, :] = jnp.zeros((tokens, width), jnp.bfloat16)

            @pl.when(me + offset < count)
            def _(offset=offset):
                copy(offset).wait_send()


def gather(keys, queries, reach, group):
    heads, width, tokens = queries.shape
    return pl.pallas_call(
        partial(gather_kernel, reach, lax.axis_size("ctx")),
        grid=(heads // group,),
        in_specs=[
            pl.BlockSpec((width, tokens), lambda i: (0, 0)),
            pl.BlockSpec((group, width, tokens), lambda i: (i, 0, 0)),
        ],
        out_specs=[
            pl.BlockSpec(((reach + 1) * tokens, width), lambda i: (0, 0)),
            pl.BlockSpec((tokens, group, width), lambda i: (0, i, 0)),
        ],
        out_shape=[
            jax.ShapeDtypeStruct(((reach + 1) * tokens, width), jnp.bfloat16),
            jax.ShapeDtypeStruct((tokens, heads, width), jnp.bfloat16),
        ],
        scratch_shapes=[
            pltpu.VMEM((reach, width, tokens), jnp.bfloat16),
            pltpu.VMEM((pl.cdiv(width, LANES), tokens * group, LANES), jnp.float32),
            pltpu.SemaphoreType.DMA((reach,)),
            pltpu.SemaphoreType.DMA((reach,)),
        ],
        compiler_params=pltpu.CompilerParams(
            dimension_semantics=("arbitrary",),
            collective_id=0,
            has_side_effects=True,
            vmem_limit_bytes=60 * 1024 * 1024,
        ),
        name="gather_relay",
    )(keys, queries)


def turn_kernel(dq_ref, out_ref, wide):
    tokens, group, width = dq_ref.shape
    for c in range(pl.cdiv(width, LANES)):
        size = min(LANES, width - c * LANES)
        part = dq_ref[:, :, c * LANES : c * LANES + size].astype(jnp.float32)
        if size < LANES:
            part = jnp.concatenate([part, jnp.zeros((tokens, group, LANES - size), jnp.float32)], axis=2)
        wide[c] = part.reshape(tokens * group, LANES)
    for h in range(group):
        for c in range(pl.cdiv(width, LANES)):
            size = min(LANES, width - c * LANES)
            part = wide[c, pl.ds(h, tokens, stride=group), :]
            out_ref[h, c * LANES : c * LANES + size, :] = part.T[:size].astype(jnp.bfloat16)


def turn(d_query, group):
    tokens, heads, width = d_query.shape
    return pl.pallas_call(
        turn_kernel,
        grid=(heads // group,),
        in_specs=[pl.BlockSpec((tokens, group, width), lambda i: (0, i, 0))],
        out_specs=pl.BlockSpec((group, width, tokens), lambda i: (i, 0, 0)),
        out_shape=jax.ShapeDtypeStruct((heads, width, tokens), jnp.bfloat16),
        scratch_shapes=[pltpu.VMEM((pl.cdiv(width, LANES), tokens * group, LANES), jnp.float32)],
        compiler_params=pltpu.CompilerParams(
            dimension_semantics=("arbitrary",), vmem_limit_bytes=60 * 1024 * 1024
        ),
        name="turn_relay",
    )(d_query)


def scatter_kernel(reach, count, head_count, part_ref, out_ref, held, send_sem, recv_sem):
    me = lax.axis_index("ctx")
    head = lax.axis_index("head")
    own_rows = out_ref.shape[0]
    block_rows = own_rows * head_count
    turns = [(offset, turn) for offset in range(reach, -1, -1) for turn in range(head_count) if offset or turn]

    def rows(offset, owner):
        start = (reach - offset) * block_rows + owner * own_rows
        return pl.ds(pl.multiple_of(start, ALIGN), own_rows)

    def copy(offset, turn):
        target = (head + turn) % head_count
        slot = offset * head_count + turn
        return pltpu.make_async_remote_copy(
            src_ref=part_ref.at[rows(offset, target), :],
            dst_ref=held.at[slot],
            send_sem=send_sem.at[slot],
            recv_sem=recv_sem.at[slot],
            device_id=at(jnp.maximum(me - offset, 0), target),
            device_id_type=pl.DeviceIdType.MESH,
        )

    greet(
        [(me >= offset, at(jnp.maximum(me - offset, 0), (head + turn) % head_count)) for offset, turn in turns]
        + [
            (
                me + offset < count,
                at(jnp.minimum(me + offset, count - 1), (head - turn + head_count) % head_count),
            )
            for offset, turn in turns
        ]
    )
    for offset, turn in turns:

        @pl.when(me >= offset)
        def _(offset=offset, turn=turn):
            copy(offset, turn).start()

    for offset, turn in turns:

        @pl.when(me + offset >= count)
        def _(offset=offset, turn=turn):
            held[offset * head_count + turn] = jnp.zeros(held.shape[1:], held.dtype)

    out_ref[...] = part_ref[rows(0, head), :].astype(jnp.float32)
    for offset, turn in turns[::-1]:

        @pl.when(me + offset < count)
        def _(offset=offset, turn=turn):
            copy(offset, turn).wait_recv()

        out_ref[...] += held[offset * head_count + turn].astype(jnp.float32)
    for offset, turn in turns:

        @pl.when(me >= offset)
        def _(offset=offset, turn=turn):
            copy(offset, turn).wait_send()


def scatter(partials, block_rows, reach):
    head_count = lax.axis_size("head")
    width = partials.shape[1]
    own_rows = block_rows // head_count
    slots = (reach + 1) * head_count
    return pl.pallas_call(
        partial(scatter_kernel, reach, lax.axis_size("ctx"), head_count),
        in_specs=[pl.BlockSpec(memory_space=pltpu.VMEM)],
        out_specs=pl.BlockSpec(memory_space=pltpu.VMEM),
        out_shape=jax.ShapeDtypeStruct((own_rows, width), jnp.float32),
        scratch_shapes=[
            pltpu.VMEM((slots, own_rows, width), jnp.bfloat16),
            pltpu.SemaphoreType.DMA((slots,)),
            pltpu.SemaphoreType.DMA((slots,)),
        ],
        compiler_params=pltpu.CompilerParams(collective_id=1, has_side_effects=True),
        name="scatter_grads",
    )(partials)


def shards(query_heads, key_latent, doc_start, out_grad):
    block_rows, head_count, width = query_heads.shape
    latent = out_grad.shape[2]
    reach = (MAXDOC + block_rows - 2) // block_rows
    group = 8
    keys, queries = gather(key_latent.T, query_heads.transpose(1, 2, 0), reach, group)
    rows = block_rows * head_count
    attention, d_query, partials = attend(
        queries.reshape(rows, width),
        out_grad.reshape(rows, latent),
        keys,
        doc_start,
        head_count,
        32,
    )
    d_key = scatter(partials, block_rows, reach)
    turned = turn(d_query.reshape(block_rows, head_count, width), group)
    return (attention.reshape(block_rows, head_count, latent), turned.transpose(2, 0, 1), d_key)


def solution(mesh):
    return jax.shard_map(
        shards,
        mesh=mesh,
        in_specs=(P("ctx", "head", None), P("ctx", None), P("ctx"), P("ctx", "head", None)),
        out_specs=(P("ctx", "head", None), P("ctx", "head", None), P(("ctx", "head"), None)),
        check_vma=False,
    )
```

```python
from functools import partial

import jax
import jax.numpy as jnp
from jax import lax
from jax.experimental import pallas as pl
from jax.experimental.pallas import tpu as pltpu
from jax.sharding import PartitionSpec as P

MAXDOC = 256
LANES = 128
ALIGN = 16

score_scale = 192 ** (-0.5)
log2_e = 1.4426950408889634


def dot(left, right, dims):
    return lax.dot_general(left, right, (dims, ((), ())), preferred_element_type=jnp.float32)


def window(first_ref, tokens, reach_rows, span, tile):
    origin = lax.axis_index("ctx") * (first_ref.shape[0]) - reach_rows
    low = (first_ref[tile * tokens] - origin) // ALIGN * ALIGN
    need = reach_rows + (tile + 1) * tokens - low
    return origin, low, need


def for_width(first_ref, tokens, reach_rows, span, tile, body):
    origin, low, need = window(first_ref, tokens, reach_rows, span, tile)
    for width in range(LANES, span + 1, LANES):
        fits = need <= width
        if width == LANES:
            chosen = fits
        elif width == span:
            chosen = need > width - LANES
        else:
            chosen = fits & (need > width - LANES)

        @pl.when(chosen)
        def _(width=width):
            start = pl.multiple_of(jnp.minimum(low, span - width), ALIGN)
            body(origin, start, width)


def probs_and_grads(first_ref, q, g, keys, bias_ref, tokens, heads, reach_rows, tile, origin, start, width):
    latent = g.shape[1]
    column = lax.broadcasted_iota(jnp.int32, (1, width), 1) + start
    for t in range(tokens):
        first = first_ref[tile * tokens + t] - origin
        own = reach_rows + tile * tokens + t
        seen = (column >= first) & (column <= own)
        bias_ref[pl.ds(t, 1), :width] = jnp.where(seen, 0.0, -jnp.inf)
    scores = dot(q, keys, ((1,), (1,))) * (score_scale * log2_e)
    scores = scores.reshape(tokens, heads, width) + bias_ref[:, :width][:, None, :]
    scores = scores.reshape(tokens * heads, width)
    top = jnp.max(scores, axis=1, keepdims=True)
    expon = jnp.exp2(scores - top)
    probs = expon * (1.0 / jnp.sum(expon, axis=1, keepdims=True))
    weights = probs.astype(jnp.bfloat16)
    dprob = dot(g, keys[:, :latent], ((1,), (1,)))
    delta = jnp.sum(probs * dprob, axis=1, keepdims=True)
    dscore = (score_scale * probs * (dprob - delta)).astype(jnp.bfloat16)
    return weights, dscore


def whole_kernel(tokens, heads, reach_rows, first_ref, q_ref, g_ref, k_ref, att_ref, dq_ref, dk_ref, bias_ref, acc_ref):
    tile = pl.program_id(0)
    span = k_ref.shape[0]
    latent = g_ref.shape[1]

    @pl.when(tile == 0)
    def _():
        acc_ref[...] = jnp.zeros_like(acc_ref)

    def body(origin, start, width):
        q = q_ref[...]
        g = g_ref[...]
        rows = pl.ds(start, width)
        keys = k_ref[rows, :]
        weights, dscore = probs_and_grads(
            first_ref, q, g, keys, bias_ref, tokens, heads, reach_rows, tile, origin, start, width
        )
        acc_ref[rows, :] += dot(dscore, q, ((0,), (0,)))
        acc_ref[rows, :latent] += dot(weights, g, ((0,), (0,)))
        att_ref[...] = dot(weights, keys[:, :latent], ((1,), (0,))).astype(att_ref.dtype)
        dq_ref[...] = dot(dscore, keys, ((1,), (0,))).astype(dq_ref.dtype)

    for_width(first_ref, tokens, reach_rows, span, tile, body)

    @pl.when(tile == pl.num_programs(0) - 1)
    def _():
        dk_ref[...] = acc_ref[...].astype(dk_ref.dtype)


def attend(q, g, keys, doc_start, heads, tokens):
    rows, width = q.shape
    latent = g.shape[1]
    span = keys.shape[0]
    block_rows = doc_start.shape[0]
    tile_rows = tokens * heads
    row_spec = lambda columns: pl.BlockSpec((tile_rows, columns), lambda i, first: (i, 0))
    full = pl.BlockSpec((span, width), lambda i, first: (0, 0))
    return pl.pallas_call(
        partial(whole_kernel, tokens, heads, span - block_rows),
        grid_spec=pltpu.PrefetchScalarGridSpec(
            num_scalar_prefetch=1,
            grid=(block_rows // tokens,),
            in_specs=[row_spec(width), row_spec(latent), full],
            out_specs=[row_spec(latent), row_spec(width), full],
            scratch_shapes=[
                pltpu.VMEM((tokens, span), jnp.float32),
                pltpu.VMEM((span, width), jnp.float32),
            ],
        ),
        out_shape=[
            jax.ShapeDtypeStruct((rows, latent), jnp.bfloat16),
            jax.ShapeDtypeStruct((rows, width), jnp.bfloat16),
            jax.ShapeDtypeStruct((span, width), jnp.bfloat16),
        ],
        compiler_params=pltpu.CompilerParams(
            dimension_semantics=("arbitrary",), vmem_limit_bytes=60 * 1024 * 1024
        ),
        name="attend",
    )(doc_start, q, g, keys)


def at(ctx_index, head_index):
    return {"ctx": ctx_index, "head": head_index}


def greet(partners):
    barrier = pltpu.get_barrier_semaphore()
    for present, place in partners:

        @pl.when(present)
        def _(place=place):
            pl.semaphore_signal(
                barrier, inc=1, device_id=place, device_id_type=pl.DeviceIdType.MESH
            )

    pl.semaphore_wait(barrier, sum(jnp.where(present, 1, 0) for present, _ in partners))


def unit(size):
    row = lax.broadcasted_iota(jnp.int32, (size, size), 0)
    column = lax.broadcasted_iota(jnp.int32, (size, size), 1)
    return (row == column).astype(jnp.bfloat16)


def gather_kernel(reach, count, k_ref, q_ref, keys_ref, out_ref, held, turned, send_sem, recv_sem):
    step = pl.program_id(0)
    me = lax.axis_index("ctx")
    head = lax.axis_index("head")
    group, width, tokens = q_ref.shape

    def copy(offset):
        return pltpu.make_async_remote_copy(
            src_ref=k_ref,
            dst_ref=held.at[offset - 1],
            send_sem=send_sem.at[offset - 1],
            recv_sem=recv_sem.at[offset - 1],
            device_id=at(jnp.minimum(me + offset, count - 1), head),
            device_id_type=pl.DeviceIdType.MESH,
        )

    offsets = range(1, reach + 1)

    @pl.when(step == 0)
    def _():
        greet(
            [(me + offset < count, at(jnp.minimum(me + offset, count - 1), head)) for offset in offsets]
            + [(me >= offset, at(jnp.maximum(me - offset, 0), head)) for offset in offsets]
        )
        for offset in offsets:

            @pl.when(me + offset < count)
            def _(offset=offset):
                copy(offset).start()

    eye = unit(tokens)
    for h in range(group):
        rows = dot(eye, q_ref[h], ((1,), (1,)))
        for c in range(pl.cdiv(width, LANES)):
            size = min(LANES, width - c * LANES)
            part = rows[:, c * LANES : c * LANES + size]
            if size < LANES:
                part = jnp.concatenate([part, jnp.zeros((tokens, LANES - size), jnp.float32)], axis=1)
            turned[c, pl.ds(h, tokens, stride=group), :] = part
    for c in range(pl.cdiv(width, LANES)):
        size = min(LANES, width - c * LANES)
        part = turned[c].reshape(tokens, group, LANES).astype(jnp.bfloat16)
        out_ref[:, :, c * LANES : c * LANES + size] = part[:, :, :size]

    @pl.when(step == pl.num_programs(0) - 1)
    def _():
        keys_ref[reach * tokens :, :] = dot(eye, k_ref[...], ((1,), (1,))).astype(jnp.bfloat16)
        for offset in offsets:
            place = pl.ds((reach - offset) * tokens, tokens)

            @pl.when(me >= offset)
            def _(offset=offset, place=place):
                copy(offset).wait_recv()
                keys_ref[place, :] = dot(eye, held[offset - 1], ((1,), (1,))).astype(jnp.bfloat16)

            @pl.when(me < offset)
            def _(place=place):
                keys_ref[place, :] = jnp.zeros((tokens, width), jnp.bfloat16)

            @pl.when(me + offset < count)
            def _(offset=offset):
                copy(offset).wait_send()


def gather(keys, queries, reach, group):
    heads, width, tokens = queries.shape
    return pl.pallas_call(
        partial(gather_kernel, reach, lax.axis_size("ctx")),
        grid=(heads // group,),
        in_specs=[
            pl.BlockSpec((width, tokens), lambda i: (0, 0)),
            pl.BlockSpec((group, width, tokens), lambda i: (i, 0, 0)),
        ],
        out_specs=[
            pl.BlockSpec(((reach + 1) * tokens, width), lambda i: (0, 0)),
            pl.BlockSpec((tokens, group, width), lambda i: (0, i, 0)),
        ],
        out_shape=[
            jax.ShapeDtypeStruct(((reach + 1) * tokens, width), jnp.bfloat16),
            jax.ShapeDtypeStruct((tokens, heads, width), jnp.bfloat16),
        ],
        scratch_shapes=[
            pltpu.VMEM((reach, width, tokens), jnp.bfloat16),
            pltpu.VMEM((pl.cdiv(width, LANES), tokens * group, LANES), jnp.float32),
            pltpu.SemaphoreType.DMA((reach,)),
            pltpu.SemaphoreType.DMA((reach,)),
        ],
        compiler_params=pltpu.CompilerParams(
            dimension_semantics=("arbitrary",),
            collective_id=0,
            has_side_effects=True,
            vmem_limit_bytes=60 * 1024 * 1024,
        ),
        name="gather_relay",
    )(keys, queries)


def scatter_kernel(reach, count, head_count, part_ref, dq_ref, out_ref, turned_ref, held, wide, send_sem, recv_sem):
    step = pl.program_id(0)
    me = lax.axis_index("ctx")
    head = lax.axis_index("head")
    own_rows = out_ref.shape[0]
    block_rows = own_rows * head_count
    turns = [(offset, turn) for offset in range(reach, -1, -1) for turn in range(head_count) if offset or turn]

    def rows(offset, owner):
        start = (reach - offset) * block_rows + owner * own_rows
        return pl.ds(pl.multiple_of(start, ALIGN), own_rows)

    def copy(offset, turn):
        target = (head + turn) % head_count
        slot = offset * head_count + turn
        return pltpu.make_async_remote_copy(
            src_ref=part_ref.at[rows(offset, target), :],
            dst_ref=held.at[slot],
            send_sem=send_sem.at[slot],
            recv_sem=recv_sem.at[slot],
            device_id=at(jnp.maximum(me - offset, 0), target),
            device_id_type=pl.DeviceIdType.MESH,
        )

    @pl.when(step == 0)
    def _():
        greet(
            [(me >= offset, at(jnp.maximum(me - offset, 0), (head + turn) % head_count)) for offset, turn in turns]
            + [
                (
                    me + offset < count,
                    at(jnp.minimum(me + offset, count - 1), (head - turn + head_count) % head_count),
                )
                for offset, turn in turns
            ]
        )
        for offset, turn in turns:

            @pl.when(me >= offset)
            def _(offset=offset, turn=turn):
                copy(offset, turn).start()

    tokens, group, width = dq_ref.shape
    for c in range(pl.cdiv(width, LANES)):
        size = min(LANES, width - c * LANES)
        part = dq_ref[:, :, c * LANES : c * LANES + size].astype(jnp.float32)
        if size < LANES:
            part = jnp.concatenate([part, jnp.zeros((tokens, group, LANES - size), jnp.float32)], axis=2)
        wide[c] = part.reshape(tokens * group, LANES)
    for h in range(group):
        for c in range(pl.cdiv(width, LANES)):
            size = min(LANES, width - c * LANES)
            part = wide[c, pl.ds(h, tokens, stride=group), :]
            turned_ref[h, c * LANES : c * LANES + size, :] = part.astype(jnp.bfloat16).T[:size]

    @pl.when(step == pl.num_programs(0) - 1)
    def _():
        for offset, turn in turns:

            @pl.when(me + offset >= count)
            def _(offset=offset, turn=turn):
                held[offset * head_count + turn] = jnp.zeros(held.shape[1:], held.dtype)

        out_ref[...] = part_ref[rows(0, head), :].astype(jnp.float32)
        for offset, turn in turns[::-1]:

            @pl.when(me + offset < count)
            def _(offset=offset, turn=turn):
                copy(offset, turn).wait_recv()

            out_ref[...] += held[offset * head_count + turn].astype(jnp.float32)
        for offset, turn in turns:

            @pl.when(me >= offset)
            def _(offset=offset, turn=turn):
                copy(offset, turn).wait_send()


def scatter(partials, d_query, block_rows, reach, group):
    head_count = lax.axis_size("head")
    tokens, heads, width = d_query.shape
    own_rows = block_rows // head_count
    slots = (reach + 1) * head_count
    return pl.pallas_call(
        partial(scatter_kernel, reach, lax.axis_size("ctx"), head_count),
        grid=(heads // group,),
        in_specs=[
            pl.BlockSpec(partials.shape, lambda i: (0, 0)),
            pl.BlockSpec((tokens, group, width), lambda i: (0, i, 0)),
        ],
        out_specs=[
            pl.BlockSpec((own_rows, width), lambda i: (0, 0)),
            pl.BlockSpec((group, width, tokens), lambda i: (i, 0, 0)),
        ],
        out_shape=[
            jax.ShapeDtypeStruct((own_rows, width), jnp.float32),
            jax.ShapeDtypeStruct((heads, width, tokens), jnp.bfloat16),
        ],
        scratch_shapes=[
            pltpu.VMEM((slots, own_rows, width), jnp.bfloat16),
            pltpu.VMEM((pl.cdiv(width, LANES), tokens * group, LANES), jnp.float32),
            pltpu.SemaphoreType.DMA((slots,)),
            pltpu.SemaphoreType.DMA((slots,)),
        ],
        compiler_params=pltpu.CompilerParams(
            dimension_semantics=("arbitrary",),
            collective_id=1,
            has_side_effects=True,
            vmem_limit_bytes=60 * 1024 * 1024,
        ),
        name="scatter_grads",
    )(partials, d_query)


def shards(query_heads, key_latent, doc_start, out_grad):
    block_rows, head_count, width = query_heads.shape
    latent = out_grad.shape[2]
    reach = (MAXDOC + block_rows - 2) // block_rows
    group = 8
    keys, queries = gather(key_latent.T, query_heads.transpose(1, 2, 0), reach, group)
    rows = block_rows * head_count
    attention, d_query, partials = attend(
        queries.reshape(rows, width),
        out_grad.reshape(rows, latent),
        keys,
        doc_start,
        head_count,
        32,
    )
    d_key, turned = scatter(
        partials, d_query.reshape(block_rows, head_count, width), block_rows, reach, group
    )
    return (attention.reshape(block_rows, head_count, latent), turned.transpose(2, 0, 1), d_key)


def solution(mesh):
    return jax.shard_map(
        shards,
        mesh=mesh,
        in_specs=(P("ctx", "head", None), P("ctx", None), P("ctx"), P("ctx", "head", None)),
        out_specs=(P("ctx", "head", None), P("ctx", "head", None), P(("ctx", "head"), None)),
        check_vma=False,
    )
```

```python
from functools import partial

import jax
import jax.numpy as jnp
from jax import lax
from jax.experimental import pallas as pl
from jax.experimental.pallas import tpu as pltpu
from jax.sharding import PartitionSpec as P

MAXDOC = 256
LANES = 128
ALIGN = 16

score_scale = 192 ** (-0.5)
log2_e = 1.4426950408889634


def dot(left, right, dims):
    return lax.dot_general(left, right, (dims, ((), ())), preferred_element_type=jnp.float32)


def window(first_ref, tokens, reach_rows, span, tile):
    origin = lax.axis_index("ctx") * (first_ref.shape[0]) - reach_rows
    low = (first_ref[tile * tokens] - origin) // ALIGN * ALIGN
    need = reach_rows + (tile + 1) * tokens - low
    return origin, low, need


def for_width(first_ref, tokens, reach_rows, span, tile, body):
    origin, low, need = window(first_ref, tokens, reach_rows, span, tile)
    for width in range(LANES, span + 1, LANES):
        fits = need <= width
        if width == LANES:
            chosen = fits
        elif width == span:
            chosen = need > width - LANES
        else:
            chosen = fits & (need > width - LANES)

        @pl.when(chosen)
        def _(width=width):
            start = pl.multiple_of(jnp.minimum(low, span - width), ALIGN)
            body(origin, start, width)


def probs_and_grads(first_ref, q, g, keys, bias_ref, tokens, heads, reach_rows, tile, origin, start, width):
    latent = g.shape[1]
    column = lax.broadcasted_iota(jnp.int32, (1, width), 1) + start
    for t in range(tokens):
        first = first_ref[tile * tokens + t] - origin
        own = reach_rows + tile * tokens + t
        seen = (column >= first) & (column <= own)
        bias_ref[pl.ds(t, 1), :width] = jnp.where(seen, 0.0, -jnp.inf)
    scores = dot(q, keys, ((1,), (1,))) * (score_scale * log2_e)
    scores = scores.reshape(tokens, heads, width) + bias_ref[:, :width][:, None, :]
    scores = scores.reshape(tokens * heads, width)
    top = jnp.max(scores, axis=1, keepdims=True)
    expon = jnp.exp2(scores - top)
    probs = expon * (1.0 / jnp.sum(expon, axis=1, keepdims=True))
    weights = probs.astype(jnp.bfloat16)
    dprob = dot(g, keys[:, :latent], ((1,), (1,)))
    delta = jnp.sum(probs * dprob, axis=1, keepdims=True)
    dscore = (score_scale * probs * (dprob - delta)).astype(jnp.bfloat16)
    return weights, dscore


def whole_kernel(tokens, heads, reach_rows, first_ref, q_ref, g_ref, k_ref, att_ref, dq_ref, dk_ref, bias_ref, acc_ref):
    tile = pl.program_id(0)
    span = k_ref.shape[0]
    latent = g_ref.shape[1]

    @pl.when(tile == 0)
    def _():
        acc_ref[...] = jnp.zeros_like(acc_ref)

    def body(origin, start, width):
        q = q_ref[...]
        g = g_ref[...]
        rows = pl.ds(start, width)
        keys = k_ref[rows, :]
        weights, dscore = probs_and_grads(
            first_ref, q, g, keys, bias_ref, tokens, heads, reach_rows, tile, origin, start, width
        )
        acc_ref[rows, :] += dot(dscore, q, ((0,), (0,)))
        acc_ref[rows, :latent] += dot(weights, g, ((0,), (0,)))
        att_ref[...] = dot(weights, keys[:, :latent], ((1,), (0,))).astype(att_ref.dtype)
        dq_ref[...] = dot(dscore, keys, ((1,), (0,))).astype(dq_ref.dtype)

    for_width(first_ref, tokens, reach_rows, span, tile, body)

    @pl.when(tile == pl.num_programs(0) - 1)
    def _():
        dk_ref[...] = acc_ref[...].astype(dk_ref.dtype)


def attend(q, g, keys, doc_start, heads, tokens):
    rows, width = q.shape
    latent = g.shape[1]
    span = keys.shape[0]
    block_rows = doc_start.shape[0]
    tile_rows = tokens * heads
    row_spec = lambda columns: pl.BlockSpec((tile_rows, columns), lambda i, first: (i, 0))
    full = pl.BlockSpec((span, width), lambda i, first: (0, 0))
    return pl.pallas_call(
        partial(whole_kernel, tokens, heads, span - block_rows),
        grid_spec=pltpu.PrefetchScalarGridSpec(
            num_scalar_prefetch=1,
            grid=(block_rows // tokens,),
            in_specs=[row_spec(width), row_spec(latent), full],
            out_specs=[row_spec(latent), row_spec(width), full],
            scratch_shapes=[
                pltpu.VMEM((tokens, span), jnp.float32),
                pltpu.VMEM((span, width), jnp.float32),
            ],
        ),
        out_shape=[
            jax.ShapeDtypeStruct((rows, latent), jnp.bfloat16),
            jax.ShapeDtypeStruct((rows, width), jnp.bfloat16),
            jax.ShapeDtypeStruct((span, width), jnp.bfloat16),
        ],
        compiler_params=pltpu.CompilerParams(
            dimension_semantics=("arbitrary",), vmem_limit_bytes=28 * 1024 * 1024
        ),
        name="attend",
    )(doc_start, q, g, keys)


def at(ctx_index, head_index):
    return {"ctx": ctx_index, "head": head_index}


def greet(partners):
    barrier = pltpu.get_barrier_semaphore()
    for present, place in partners:

        @pl.when(present)
        def _(place=place):
            pl.semaphore_signal(
                barrier, inc=1, device_id=place, device_id_type=pl.DeviceIdType.MESH
            )

    pl.semaphore_wait(barrier, sum(jnp.where(present, 1, 0) for present, _ in partners))


def unit(size):
    row = lax.broadcasted_iota(jnp.int32, (size, size), 0)
    column = lax.broadcasted_iota(jnp.int32, (size, size), 1)
    return (row == column).astype(jnp.bfloat16)


def gather_kernel(reach, count, k_ref, q_ref, keys_ref, out_ref, held, turned, send_sem, recv_sem):
    step = pl.program_id(0)
    me = lax.axis_index("ctx")
    head = lax.axis_index("head")
    group, width, tokens = q_ref.shape

    def copy(offset):
        return pltpu.make_async_remote_copy(
            src_ref=k_ref,
            dst_ref=held.at[offset - 1],
            send_sem=send_sem.at[offset - 1],
            recv_sem=recv_sem.at[offset - 1],
            device_id=at(jnp.minimum(me + offset, count - 1), head),
            device_id_type=pl.DeviceIdType.MESH,
        )

    offsets = range(1, reach + 1)

    @pl.when(step == 0)
    def _():
        greet(
            [(me + offset < count, at(jnp.minimum(me + offset, count - 1), head)) for offset in offsets]
            + [(me >= offset, at(jnp.maximum(me - offset, 0), head)) for offset in offsets]
        )
        for offset in offsets:

            @pl.when(me + offset < count)
            def _(offset=offset):
                copy(offset).start()

    eye = unit(tokens)
    for h in range(group):
        rows = dot(eye, q_ref[h], ((1,), (1,)))
        for c in range(pl.cdiv(width, LANES)):
            size = min(LANES, width - c * LANES)
            part = rows[:, c * LANES : c * LANES + size]
            if size < LANES:
                part = jnp.concatenate([part, jnp.zeros((tokens, LANES - size), jnp.float32)], axis=1)
            turned[c, pl.ds(h, tokens, stride=group), :] = part
    for c in range(pl.cdiv(width, LANES)):
        size = min(LANES, width - c * LANES)
        part = turned[c].reshape(tokens, group, LANES).astype(jnp.bfloat16)
        out_ref[:, :, c * LANES : c * LANES + size] = part[:, :, :size]

    @pl.when(step == pl.num_programs(0) - 1)
    def _():
        keys_ref[reach * tokens :, :] = dot(eye, k_ref[...], ((1,), (1,))).astype(jnp.bfloat16)
        for offset in offsets:
            place = pl.ds((reach - offset) * tokens, tokens)

            @pl.when(me >= offset)
            def _(offset=offset, place=place):
                copy(offset).wait_recv()
                keys_ref[place, :] = dot(eye, held[offset - 1], ((1,), (1,))).astype(jnp.bfloat16)

            @pl.when(me < offset)
            def _(place=place):
                keys_ref[place, :] = jnp.zeros((tokens, width), jnp.bfloat16)

            @pl.when(me + offset < count)
            def _(offset=offset):
                copy(offset).wait_send()


def gather(keys, queries, reach, group):
    heads, width, tokens = queries.shape
    return pl.pallas_call(
        partial(gather_kernel, reach, lax.axis_size("ctx")),
        grid=(heads // group,),
        in_specs=[
            pl.BlockSpec((width, tokens), lambda i: (0, 0)),
            pl.BlockSpec((group, width, tokens), lambda i: (i, 0, 0)),
        ],
        out_specs=[
            pl.BlockSpec(((reach + 1) * tokens, width), lambda i: (0, 0)),
            pl.BlockSpec((tokens, group, width), lambda i: (0, i, 0)),
        ],
        out_shape=[
            jax.ShapeDtypeStruct(((reach + 1) * tokens, width), jnp.bfloat16),
            jax.ShapeDtypeStruct((tokens, heads, width), jnp.bfloat16),
        ],
        scratch_shapes=[
            pltpu.VMEM((reach, width, tokens), jnp.bfloat16),
            pltpu.VMEM((pl.cdiv(width, LANES), tokens * group, LANES), jnp.float32),
            pltpu.SemaphoreType.DMA((reach,)),
            pltpu.SemaphoreType.DMA((reach,)),
        ],
        compiler_params=pltpu.CompilerParams(
            dimension_semantics=("arbitrary",),
            collective_id=0,
            has_side_effects=True,
            vmem_limit_bytes=28 * 1024 * 1024,
        ),
        name="gather_relay",
    )(keys, queries)


def scatter_kernel(reach, count, head_count, part_ref, dq_ref, out_ref, turned_ref, held, wide, send_sem, recv_sem):
    step = pl.program_id(0)
    me = lax.axis_index("ctx")
    head = lax.axis_index("head")
    own_rows = out_ref.shape[0]
    block_rows = own_rows * head_count
    turns = [(offset, turn) for offset in range(reach, -1, -1) for turn in range(head_count) if offset or turn]

    def rows(offset, owner):
        start = (reach - offset) * block_rows + owner * own_rows
        return pl.ds(pl.multiple_of(start, ALIGN), own_rows)

    def copy(offset, turn):
        target = (head + turn) % head_count
        slot = offset * head_count + turn
        return pltpu.make_async_remote_copy(
            src_ref=part_ref.at[rows(offset, target), :],
            dst_ref=held.at[slot],
            send_sem=send_sem.at[slot],
            recv_sem=recv_sem.at[slot],
            device_id=at(jnp.maximum(me - offset, 0), target),
            device_id_type=pl.DeviceIdType.MESH,
        )

    @pl.when(step == 0)
    def _():
        greet(
            [(me >= offset, at(jnp.maximum(me - offset, 0), (head + turn) % head_count)) for offset, turn in turns]
            + [
                (
                    me + offset < count,
                    at(jnp.minimum(me + offset, count - 1), (head - turn + head_count) % head_count),
                )
                for offset, turn in turns
            ]
        )
        for offset, turn in turns:

            @pl.when(me >= offset)
            def _(offset=offset, turn=turn):
                copy(offset, turn).start()

    tokens, group, width = dq_ref.shape
    for c in range(pl.cdiv(width, LANES)):
        size = min(LANES, width - c * LANES)
        part = dq_ref[:, :, c * LANES : c * LANES + size].astype(jnp.float32)
        if size < LANES:
            part = jnp.concatenate([part, jnp.zeros((tokens, group, LANES - size), jnp.float32)], axis=2)
        wide[c] = part.reshape(tokens * group, LANES)
    for h in range(group):
        for c in range(pl.cdiv(width, LANES)):
            size = min(LANES, width - c * LANES)
            part = wide[c, pl.ds(h, tokens, stride=group), :]
            turned_ref[h, c * LANES : c * LANES + size, :] = part.astype(jnp.bfloat16).T[:size]

    @pl.when(step == pl.num_programs(0) - 1)
    def _():
        for offset, turn in turns:

            @pl.when(me + offset >= count)
            def _(offset=offset, turn=turn):
                held[offset * head_count + turn] = jnp.zeros(held.shape[1:], held.dtype)

        out_ref[...] = part_ref[rows(0, head), :].astype(jnp.float32)
        for offset, turn in turns[::-1]:

            @pl.when(me + offset < count)
            def _(offset=offset, turn=turn):
                copy(offset, turn).wait_recv()

            out_ref[...] += held[offset * head_count + turn].astype(jnp.float32)
        for offset, turn in turns:

            @pl.when(me >= offset)
            def _(offset=offset, turn=turn):
                copy(offset, turn).wait_send()


def scatter(partials, d_query, block_rows, reach, group):
    head_count = lax.axis_size("head")
    tokens, heads, width = d_query.shape
    own_rows = block_rows // head_count
    slots = (reach + 1) * head_count
    return pl.pallas_call(
        partial(scatter_kernel, reach, lax.axis_size("ctx"), head_count),
        grid=(heads // group,),
        in_specs=[
            pl.BlockSpec(partials.shape, lambda i: (0, 0)),
            pl.BlockSpec((tokens, group, width), lambda i: (0, i, 0)),
        ],
        out_specs=[
            pl.BlockSpec((own_rows, width), lambda i: (0, 0)),
            pl.BlockSpec((group, width, tokens), lambda i: (i, 0, 0)),
        ],
        out_shape=[
            jax.ShapeDtypeStruct((own_rows, width), jnp.float32),
            jax.ShapeDtypeStruct((heads, width, tokens), jnp.bfloat16),
        ],
        scratch_shapes=[
            pltpu.VMEM((slots, own_rows, width), jnp.bfloat16),
            pltpu.VMEM((pl.cdiv(width, LANES), tokens * group, LANES), jnp.float32),
            pltpu.SemaphoreType.DMA((slots,)),
            pltpu.SemaphoreType.DMA((slots,)),
        ],
        compiler_params=pltpu.CompilerParams(
            dimension_semantics=("arbitrary",),
            collective_id=1,
            has_side_effects=True,
            vmem_limit_bytes=28 * 1024 * 1024,
        ),
        name="scatter_grads",
    )(partials, d_query)


def shards(query_heads, key_latent, doc_start, out_grad):
    block_rows, head_count, width = query_heads.shape
    latent = out_grad.shape[2]
    reach = (MAXDOC + block_rows - 2) // block_rows
    group = 8
    keys, queries = gather(key_latent.T, query_heads.transpose(1, 2, 0), reach, group)
    rows = block_rows * head_count
    attention, d_query, partials = attend(
        queries.reshape(rows, width),
        out_grad.reshape(rows, latent),
        keys,
        doc_start,
        head_count,
        32,
    )
    d_key, turned = scatter(
        partials, d_query.reshape(block_rows, head_count, width), block_rows, reach, group
    )
    return (attention.reshape(block_rows, head_count, latent), turned.transpose(2, 0, 1), d_key)


def solution(mesh):
    return jax.shard_map(
        shards,
        mesh=mesh,
        in_specs=(P("ctx", "head", None), P("ctx", None), P("ctx"), P("ctx", "head", None)),
        out_specs=(P("ctx", "head", None), P("ctx", "head", None), P(("ctx", "head"), None)),
        check_vma=False,
    )
```
